32 devices in a mesh: groups: 2 (over x), gx: 16 (over z, y, core).
Axes of the slice: x: 2, y: 2, z: 4, core: 2. Of those that a mesh axis runs over, the one named last changes fastest.
Arguments:
- snapshots: bfloat16 [256, 4, 512, 128], P('gx', None, 'groups'), parts along dimension 2, may hold values from -20 to 20
- cell_weights: float32 [512, 128], P(('groups', 'gx')), parts along dimension 0, may hold values from 0.5 to 4.5
- diffusivity: float32 [4, 512, 128], P(None, ('groups', 'gx')), parts along dimension 1, may hold values from 0.2 to 2
Outputs:
- diffused_modes: bfloat16 [256, 4, 512, 128], P(None, None, ('groups', 'gx')), parts along dimension 2
- reduced_operator: float32 [512, 256], P('groups'), parts along dimension 0
The draws below stay inside these ranges and needn't reach their ends.
There are 2 independent parts, one for each index of `groups`. The reference program is written for one: setup_inputs(seed, part) draws one part's arguments, and reference() takes and returns one part's arrays. A program takes and returns all parts, laid end to end along the dimension named above; each array names one. Nothing has to cross between parts.
All inputs are finite; a program needn't handle non-finite values.
Results may differ from the reference program's by a relative error of at most 0.0005.
Values may be sent and summed in bfloat16 or wider, within the bound.
A program may use at most 128 MiB of HBM per device.

```python
import math
import jax
import jax.numpy as jnp
from jax import lax

S = 256
V = 4
PY = 128
NX = 256


def draw_snapshots(key, part):
    keys = jax.random.split(key, 4)
    amplitude = jnp.exp(jax.random.uniform(keys[0], (S, 1, 1, 1), minval=0.0, maxval=math.log(3.0)))
    noise = jax.random.truncated_normal(keys[1], -4.0, 4.0, (S, V, NX, PY))
    coeffs = jax.random.uniform(keys[2], (4, S, 1, 1, 1), minval=-0.6, maxval=0.6)
    pattern = jax.random.uniform(keys[3], (4, 1, V, NX, PY), minval=-1.0, maxval=1.0)
    shared = coeffs[0] * pattern[0] + coeffs[1] * pattern[1] + coeffs[2] * pattern[2] + coeffs[3] * pattern[3]
    return (amplitude * (noise + shared)).astype(jnp.bfloat16)


def draw_cell_weights(key, part):
    ramp = 1.0 + 2.0 * jnp.arange(NX, dtype=jnp.float32)[:, None] / (NX - 1)
    factor = jax.random.uniform(key, (NX, PY), minval=0.5, maxval=1.5)
    return ramp * factor


def shard_levels(rng, extent, shards, smallest, largest):
    def one(axis_at, parts):
        heights = jax.random.uniform(jax.random.fold_in(jax.random.fold_in(rng, 6), axis_at), (parts,), jnp.float32, smallest / len(shards), largest / len(shards))
        return jnp.repeat(jnp.exp(heights), extent[axis_at] // parts).reshape((-1,) + (1,) * (len(extent) - axis_at - 1))

    level = one(*shards[0])
    for cut in shards[1:]:
        level = level * one(*cut)
    return level


def setup_inputs(seed: int = 0, part: int = 0) -> dict:
    arg_keys = jax.random.split(jax.random.key(seed), 4)
    own_keys = jax.random.split(jax.random.fold_in(arg_keys[3], part), 4)
    snapshots = draw_snapshots(jax.random.fold_in(jax.random.fold_in(arg_keys[3], part), 71), part)
    cell_weights = draw_cell_weights(jax.random.fold_in(jax.random.fold_in(arg_keys[3], part), 71), part)
    diffusivity = jnp.clip(jnp.exp(math.log(2.0) - 2.3025851 * jax.random.uniform(own_keys[2], (V, NX, PY), jnp.float32) ** shard_levels(own_keys[2], (V, NX, PY), ((1, 16),), -0.2, 0.2)), 0.2, 2.0)
    return {"snapshots": snapshots, "cell_weights": cell_weights, "diffusivity": diffusivity}


def stencil_apply(padded_x, diffusivity):
    field = padded_x[:, :, 2:-2]
    along_x = (-padded_x[:, :, :-4] + 16.0 * padded_x[:, :, 1:-3] - 30.0 * field + 16.0 * padded_x[:, :, 3:-1] - padded_x[:, :, 4:]) / 12.0
    padded_y = jnp.pad(field, ((0, 0), (0, 0), (0, 0), (2, 2)))
    along_y = (-padded_y[..., :-4] + 16.0 * padded_y[..., 1:-3] - 30.0 * field + 16.0 * padded_y[..., 3:-1] - padded_y[..., 4:]) / 12.0
    return diffusivity * (along_x + along_y)

def reference(snapshots, cell_weights, diffusivity):
    hi = lax.Precision.HIGHEST
    cell_count = snapshots.shape[1] * snapshots.shape[2] * snapshots.shape[3]
    snap_float = snapshots.astype(jnp.float32)
    gram_total = jnp.einsum('svxy,tvxy->st', snap_float, snap_float * cell_weights, precision=hi) / cell_count
    lower_factor = jnp.linalg.cholesky(gram_total)
    identity = jnp.eye(gram_total.shape[0], dtype=jnp.float32)
    rotation = jax.scipy.linalg.solve_triangular(lower_factor, identity, lower=True)
    mode_field = jnp.einsum('st,tvxy->svxy', rotation, snap_float, precision=hi)
    padded_x = jnp.pad(mode_field, ((0, 0), (0, 0), (2, 2), (0, 0)))
    diffused = stencil_apply(padded_x, diffusivity)
    reduced = jnp.einsum('svxy,tvxy->st', mode_field * cell_weights, diffused, precision=hi) / cell_count
    return (diffused.astype(jnp.bfloat16), reduced)
```

```python
import functools

import jax
import jax.numpy as jnp
from jax import lax
from jax.experimental import pallas as pl
from jax.experimental.pallas import tpu as pltpu
from jax.sharding import PartitionSpec as P

MESH = pl.DeviceIdType.MESH
HIGHEST = lax.Precision.HIGHEST
NT = (((1,), (1,)), ((), ()))
TN = (((0,), (0,)), ((), ()))
PACK = 16
PIVOTS = 32


def iota(shape, dim):
    return lax.broadcasted_iota(jnp.int32, shape, dim)


def swap_matrix(outer, inner):
    size = outer * inner
    row, col = iota((size, size), 0), iota((size, size), 1)
    source = lax.rem(row, inner) * outer + lax.div(row, inner)
    return jnp.where(col == source, 1.0, 0.0).astype(jnp.bfloat16)


def parts_of(value, count):
    parts = []
    for _ in range(count):
        part = value.astype(jnp.bfloat16)
        parts.append(part)
        value = value - part.astype(jnp.float32)
    return parts


def dot32(a, b, dims):
    return lax.dot_general(a, b, dims, preferred_element_type=jnp.float32)


def gather_kernel(n, snap_ref, weight_ref, diff_ref, x_ref, gram_ref, cross_ref,
                  pod, local_sem, send_sem, recv_sem, halo_send, halo_recv):
    me = lax.axis_index("gx")
    own, variables, _, cols = snap_ref.shape
    total, rows = pod.shape[0], pod.shape[2]

    barrier = pltpu.get_barrier_semaphore()

    def greet(k, carry):
        pl.semaphore_signal(
            barrier, inc=1, device_id={"gx": lax.rem(me + k, n)}, device_id_type=MESH
        )
        return carry

    lax.fori_loop(1, n, greet, 0)

    def own_copy(v):
        return pltpu.make_async_copy(
            snap_ref.at[:, v, pl.ds(me * rows, rows)],
            pod.at[pl.ds(me * own, own), v],
            local_sem.at[v],
        )

    for v in range(variables):
        own_copy(v).start()
    pl.semaphore_wait(barrier, n - 1)

    for v in range(variables):

        def send(k, carry, v=v):
            offset = lax.div(k, 2) + lax.rem(k, 2) * (n // 2)
            target = lax.rem(me + offset, n)
            pltpu.make_async_remote_copy(
                src_ref=snap_ref.at[:, v, pl.ds(target * rows, rows)],
                dst_ref=pod.at[pl.ds(me * own, own), v],
                send_sem=send_sem.at[v],
                recv_sem=recv_sem.at[v],
                device_id={"gx": target},
                device_id_type=MESH,
            ).start()
            return carry

        lax.fori_loop(1, n, send, 0)

    gram_ref[...] = jnp.zeros_like(gram_ref)
    cross_ref[...] = jnp.zeros_like(cross_ref)
    lane_gap = iota((cols, cols), 0) - iota((cols, cols), 1)
    band = jnp.where(lane_gap == 0, -60.0, 0.0)
    band = jnp.where(jnp.abs(lane_gap) == 1, 16.0, band)
    band = jnp.where(jnp.abs(lane_gap) == 2, -1.0, band).astype(jnp.bfloat16)
    swap = swap_matrix(rows, PACK)

    def all_but_own(v, sem):
        piece = pod.at[pl.ds(0, total - own), v]
        return pltpu.make_async_copy(piece, piece, sem.at[v])

    def to_low(v):
        return pltpu.make_async_remote_copy(
            src_ref=x_ref.at[v, pl.ds(2, 2)],
            dst_ref=x_ref.at[v, pl.ds(rows + 2, 2)],
            send_sem=halo_send.at[0, v],
            recv_sem=halo_recv.at[0, v],
            device_id={"gx": jnp.maximum(me - 1, 0)},
            device_id_type=MESH,
        )

    def to_high(v):
        return pltpu.make_async_remote_copy(
            src_ref=x_ref.at[v, pl.ds(rows, 2)],
            dst_ref=x_ref.at[v, pl.ds(0, 2)],
            send_sem=halo_send.at[1, v],
            recv_sem=halo_recv.at[1, v],
            device_id={"gx": jnp.minimum(me + 1, n - 1)},
            device_id_type=MESH,
        )

    for v in range(variables):
        own_copy(v).wait()
        all_but_own(v, recv_sem).wait()

        @pl.loop(0, total // PACK)
        def _(g):
            first = pl.multiple_of(g * PACK, PACK)
            block = pod[pl.ds(first, PACK), v].reshape(PACK * rows, cols)
            turned = dot32(swap, block, (((1,), (0,)), ((), ())))
            x_ref[v, pl.ds(2, rows), pl.ds(first, PACK), :] = turned.astype(
                jnp.bfloat16
            ).reshape(rows, PACK, cols)

        @pl.when(me > 0)
        def _():
            to_low(v).start()

        @pl.when(me < n - 1)
        def _():
            to_high(v).start()

        @pl.when(me == 0)
        def _():
            x_ref[v, 0:2] = jnp.zeros((2, total, cols), jnp.bfloat16)

        @pl.when(me == n - 1)
        def _():
            x_ref[v, rows + 2 : rows + 4] = jnp.zeros((2, total, cols), jnp.bfloat16)

        @pl.loop(0, rows // 2)
        def _(pair):
            at = 2 * pair
            plain, weighed = [], []
            for step in range(2):
                field = x_ref[v, at + step + 2]
                plain.append(field)
                weighed.append(field.astype(jnp.float32) * weight_ref[pl.ds(at + step, 1), :])
            left = jnp.concatenate(plain, axis=1)
            acc = gram_ref[...]
            for part in parts_of(jnp.concatenate(weighed, axis=1), 3):
                acc += dot32(left, part, NT)
            gram_ref[...] = acc

        @pl.when(me < n - 1)
        def _():
            to_low(v).wait_recv()
            to_high(v).wait_send()

        @pl.when(me > 0)
        def _():
            to_high(v).wait_recv()
            to_low(v).wait_send()

        @pl.loop(0, rows // 2)
        def _(pair):
            at = 2 * pair
            plain, weighed = [], []
            for step in range(2):
                near = [x_ref[v, at + step + k] for k in range(5)]
                wide = [near[k].astype(jnp.float32) for k in (0, 1, 3, 4)]
                spread = dot32(near[2], band, (((1,), (0,)), ((), ())))
                spread += 16.0 * (wide[1] + wide[2]) - (wide[0] + wide[3])
                scale = weight_ref[pl.ds(at + step, 1), :] * diff_ref[v, pl.ds(at + step, 1), :]
                plain.append(near[2])
                weighed.append(spread * (scale / 12.0))
            left = jnp.concatenate(plain, axis=1)
            acc = cross_ref[...]
            for part in parts_of(jnp.concatenate(weighed, axis=1), 3):
                acc += dot32(left, part, NT)
            cross_ref[...] = acc

    for v in range(variables):
        all_but_own(v, send_sem).wait()


def gather(n, snapshots, cell_weights, diffusivity):
    own, variables, _, cols = snapshots.shape
    rows = cell_weights.shape[0]
    total = own * n
    vmem = pl.BlockSpec(memory_space=pltpu.VMEM)
    square = jax.ShapeDtypeStruct((total, total), jnp.float32)
    return pl.pallas_call(
        functools.partial(gather_kernel, n),
        out_shape=(
            jax.ShapeDtypeStruct((variables, rows + 4, total, cols), jnp.bfloat16),
            square,
            square,
        ),
        in_specs=[pl.BlockSpec(memory_space=pl.ANY), vmem, vmem],
        out_specs=(vmem, vmem, vmem),
        scratch_shapes=[
            pltpu.VMEM((total, variables, rows, cols), jnp.bfloat16),
            pltpu.SemaphoreType.DMA((variables,)),
            pltpu.SemaphoreType.DMA((variables,)),
            pltpu.SemaphoreType.DMA((variables,)),
            pltpu.SemaphoreType.DMA((2, variables)),
            pltpu.SemaphoreType.DMA((2, variables)),
        ],
        compiler_params=pltpu.CompilerParams(collective_id=0, has_side_effects=True),
        name="gather",
    )(snapshots, cell_weights, diffusivity)


def factor_kernel(cells, gram_ref, cross_ref, rotation_ref, reduced_ref, work):
    size = gram_ref.shape[0]
    lanes = 128
    work[:, :size] = gram_ref[...] * (1.0 / cells)
    work[:, size:] = jnp.where(iota((size, size), 0) == iota((size, size), 1), 1.0, 0.0)
    row = iota((PIVOTS, lanes), 0)
    lane = iota((PIVOTS, lanes), 1)
    for first in range(0, size, PIVOTS):
        group, shift = first // lanes * lanes, first % lanes
        block = work[first : first + PIVOTS, group : group + lanes]
        if shift:
            block = pltpu.roll(block, lanes - shift, 1)
        block = jnp.where(lane < PIVOTS, block, jnp.where(lane == row + PIVOTS, 1.0, 0.0))
        for k in range(PIVOTS):
            pivot_row = block[k : k + 1, :]
            scaled = pivot_row * (1.0 / pivot_row[:, k : k + 1])
            column = jnp.where(row > k, block[:, k : k + 1], 0.0)
            block = block - column * scaled
        pivots = jnp.sum(jnp.where(lane == row, block, 0.0), axis=1, keepdims=True)
        inverse = pltpu.roll(block, lanes - PIVOTS, 1) / jnp.sqrt(pivots)
        stripe = jnp.dot(
            inverse[:, :PIVOTS],
            work[first : first + PIVOTS, :],
            precision=HIGHEST,
            preferred_element_type=jnp.float32,
        )
        rotation_ref[first : first + PIVOTS, :] = stripe[:, size:]
        if first + PIVOTS < size:
            work[...] -= lax.dot_general(
                stripe[:, :size],
                stripe,
                TN,
                precision=HIGHEST,
                preferred_element_type=jnp.float32,
            )
    rotation = rotation_ref[...]
    half = jnp.dot(
        rotation, cross_ref[...] * (1.0 / cells), precision=HIGHEST,
        preferred_element_type=jnp.float32,
    )
    reduced_ref[...] = lax.dot_general(
        half, rotation, NT, precision=HIGHEST, preferred_element_type=jnp.float32
    )


def factor(cells, gram, cross):
    size = gram.shape[0]
    vmem = pl.BlockSpec(memory_space=pltpu.VMEM)
    square = jax.ShapeDtypeStruct((size, size), jnp.float32)
    return pl.pallas_call(
        functools.partial(factor_kernel, float(cells)),
        out_shape=(square, square),
        in_specs=[vmem, vmem],
        out_specs=(vmem, vmem),
        scratch_shapes=[pltpu.VMEM((size, 2 * size), jnp.float32)],
        name="factor",
    )(gram, cross)


def modes_kernel(rotation_ref, diff_ref, x_ref, out_ref, field, turned):
    rows, cols = diff_ref.shape[1:]
    total = rotation_ref.shape[0]
    parts = parts_of(rotation_ref[...], 3)
    lane = iota((1, cols), 1)
    masks = {
        shift: jnp.where(
            (lane >= shift) & (lane < cols + shift), -1.0 if abs(shift) == 2 else 16.0, 0.0
        )
        for shift in (-2, -1, 1, 2)
    }

    @pl.loop(0, (rows + 4) // 2)
    def _(pair):
        right = jnp.concatenate([x_ref[0, 2 * pair], x_ref[0, 2 * pair + 1]], axis=1)
        acc = dot32(parts[0], right, (((1,), (0,)), ((), ())))
        for part in parts[1:]:
            acc += dot32(part, right, (((1,), (0,)), ((), ())))
        field[2 * pair] = acc[:, :cols]
        field[2 * pair + 1] = acc[:, cols:]

    @pl.loop(0, rows)
    def _(at):
        near = [field[at + k] for k in range(5)]
        spread = 16.0 * (near[1] + near[3]) - (near[0] + near[4]) - 60.0 * near[2]
        for shift in (-2, -1, 1, 2):
            spread += pltpu.roll(near[2], shift % cols, 1) * masks[shift]
        spread = spread * (diff_ref[0, pl.ds(at, 1), :] / 12.0)
        turned[at] = spread.astype(jnp.bfloat16)

    swap = swap_matrix(PACK, rows)

    @pl.loop(0, total // PACK)
    def _(g):
        first = pl.multiple_of(g * PACK, PACK)
        block = turned[:, pl.ds(first, PACK), :].reshape(rows * PACK, cols)
        out_ref[pl.ds(first, PACK), 0] = (
            dot32(swap, block, (((1,), (0,)), ((), ())))
            .astype(jnp.bfloat16)
            .reshape(PACK, rows, cols)
        )


def modes(rotation, diffusivity, fields):
    variables, rows, cols = diffusivity.shape
    total = rotation.shape[0]
    return pl.pallas_call(
        modes_kernel,
        out_shape=jax.ShapeDtypeStruct((total, variables, rows, cols), jnp.bfloat16),
        grid=(variables,),
        in_specs=[
            pl.BlockSpec((total, total), lambda v: (0, 0)),
            pl.BlockSpec((1, rows, cols), lambda v: (v, 0, 0)),
            pl.BlockSpec((1, rows + 4, total, cols), lambda v: (v, 0, 0, 0)),
        ],
        out_specs=pl.BlockSpec((total, 1, rows, cols), lambda v: (0, v, 0, 0)),
        scratch_shapes=[
            pltpu.VMEM((rows + 4, total, cols), jnp.float32),
            pltpu.VMEM((rows, total, cols), jnp.bfloat16),
        ],
        name="modes",
    )(rotation, diffusivity, fields)


def on_device(n, snapshots, cell_weights, diffusivity):
    variables, rows, cols = diffusivity.shape
    fields, gram, cross = gather(n, snapshots, cell_weights, diffusivity)
    gram, cross = lax.psum((gram, cross), "gx")
    rotation, reduced = factor(variables * rows * cols * n, gram, cross)
    return modes(rotation, diffusivity, fields), reduced


def solution(mesh):
    in_specs = (
        P("gx", None, "groups", None),
        P(("groups", "gx"), None),
        P(None, ("groups", "gx"), None),
    )
    out_specs = (P(None, None, ("groups", "gx"), None), P("groups", None))
    return jax.shard_map(
        functools.partial(on_device, mesh.shape["gx"]),
        mesh=mesh, in_specs=in_specs, out_specs=out_specs, check_vma=False,
    )
```

```python
import functools

import jax
import jax.numpy as jnp
from jax import lax
from jax.experimental import pallas as pl
from jax.experimental.pallas import tpu as pltpu
from jax.sharding import PartitionSpec as P

MESH = pl.DeviceIdType.MESH
HIGHEST = lax.Precision.HIGHEST
NT = (((1,), (1,)), ((), ()))
TN = (((0,), (0,)), ((), ()))
PACK = 16
PIVOTS = 32
PANEL = 8


def iota(shape, dim):
    return lax.broadcasted_iota(jnp.int32, shape, dim)


def swap_matrix(outer, inner):
    size = outer * inner
    row, col = iota((size, size), 0), iota((size, size), 1)
    source = lax.rem(row, inner) * outer + lax.div(row, inner)
    return jnp.where(col == source, 1.0, 0.0).astype(jnp.bfloat16)


def parts_of(value, count):
    parts = []
    for _ in range(count):
        part = value.astype(jnp.bfloat16)
        parts.append(part)
        value = value - part.astype(jnp.float32)
    return parts


def dot32(a, b, dims):
    return lax.dot_general(a, b, dims, preferred_element_type=jnp.float32)


NN = (((1,), (0,)), ((), ()))


def gather_kernel(n, snap_ref, weight_ref, diff_ref, x_ref, sums_ref,
                  pod, parts, part_sums, half, pieces,
                  local_sem, send_sem, recv_sem, halo_send, halo_recv, sum_send, sum_recv):
    me = lax.axis_index("gx")
    own, variables, _, cols = snap_ref.shape
    total, rows = pod.shape[0], pod.shape[2]
    gram_ref, cross_ref = part_sums.at[0], part_sums.at[1]

    barrier = pltpu.get_barrier_semaphore()

    def greet(k, carry):
        pl.semaphore_signal(
            barrier, inc=1, device_id={"gx": lax.rem(me + k, n)}, device_id_type=MESH
        )
        return carry

    lax.fori_loop(1, n, greet, 0)

    def own_copy(v):
        return pltpu.make_async_copy(
            snap_ref.at[:, v, pl.ds(me * rows, rows)],
            pod.at[pl.ds(me * own, own), v],
            local_sem.at[v],
        )

    def send_all(v):
        def send(k, carry):
            offset = lax.div(k, 2) + lax.rem(k, 2) * (n // 2)
            target = lax.rem(me + offset, n)
            pltpu.make_async_remote_copy(
                src_ref=snap_ref.at[:, v, pl.ds(target * rows, rows)],
                dst_ref=pod.at[pl.ds(me * own, own), v],
                send_sem=send_sem.at[v],
                recv_sem=recv_sem.at[v],
                device_id={"gx": target},
                device_id_type=MESH,
            ).start()
            return carry

        lax.fori_loop(1, n, send, 0)

    for v in range(variables):
        own_copy(v).start()
    pl.semaphore_wait(barrier, n - 1)
    ahead = min(2, variables)
    for v in range(ahead):
        send_all(v)

    part_sums[...] = jnp.zeros_like(part_sums)
    lane_gap = iota((cols, cols), 0) - iota((cols, cols), 1)
    band = jnp.where(lane_gap == 0, -60.0, 0.0)
    band = jnp.where(jnp.abs(lane_gap) == 1, 16.0, band)
    band = jnp.where(jnp.abs(lane_gap) == 2, -1.0, band).astype(jnp.bfloat16)
    swap = swap_matrix(rows, PACK)

    def all_but_own(v, sem):
        piece = pod.at[pl.ds(0, total - own), v]
        return pltpu.make_async_copy(piece, piece, sem.at[v])

    def strip(v, first, count):
        return x_ref.at[v, :, pl.ds(first * cols, count * cols)]

    def to_low(v):
        return pltpu.make_async_remote_copy(
            src_ref=strip(v, 2, 2),
            dst_ref=strip(v, rows + 2, 2),
            send_sem=halo_send.at[0, v],
            recv_sem=halo_recv.at[0, v],
            device_id={"gx": jnp.maximum(me - 1, 0)},
            device_id_type=MESH,
        )

    def to_high(v):
        return pltpu.make_async_remote_copy(
            src_ref=strip(v, rows, 2),
            dst_ref=strip(v, 0, 2),
            send_sem=halo_send.at[1, v],
            recv_sem=halo_recv.at[1, v],
            device_id={"gx": jnp.minimum(me + 1, n - 1)},
            device_id_type=MESH,
        )

    def relayout(v):
        for g in range(0, total // PACK, 2):
            blocks = [
                pod[PACK * (g + h) : PACK * (g + h + 1), v].reshape(PACK * rows, cols)
                for h in range(2)
            ]
            turned = dot32(swap, jnp.concatenate(blocks, axis=1), NN).astype(jnp.bfloat16)
            for h in range(2):
                for at in range(rows):
                    x_ref[v, PACK * (g + h) : PACK * (g + h + 1), (at + 2) * cols : (at + 3) * cols] = (
                        turned[at * PACK : (at + 1) * PACK, h * cols : (h + 1) * cols]
                    )

    def accumulate(v, acc_ref):
        left = x_ref[v, :, 2 * cols : (rows + 2) * cols]
        acc = acc_ref[...]
        for p in range(3):
            acc += dot32(left, parts[p], NT)
        acc_ref[...] = acc

    def store_parts(at, value):
        for p, part in enumerate(parts_of(value, 3)):
            parts[p, :, at * cols : (at + 1) * cols] = part

    def gram(v):
        for at in range(rows):
            field = x_ref[v, :, (at + 2) * cols : (at + 3) * cols].astype(jnp.float32)
            store_parts(at, field * weight_ref[at : at + 1, :])
        accumulate(v, gram_ref)

    def cross(v):
        @pl.when(me < n - 1)
        def _():
            to_low(v).wait_recv()
            to_high(v).wait_send()

        @pl.when(me > 0)
        def _():
            to_high(v).wait_recv()
            to_low(v).wait_send()

        for at in range(rows):
            near = [x_ref[v, :, (at + k) * cols : (at + k + 1) * cols] for k in range(5)]
            wide = [near[k].astype(jnp.float32) for k in (0, 1, 3, 4)]
            spread = dot32(near[2], band, NN)
            spread += 16.0 * (wide[1] + wide[2]) - (wide[0] + wide[3])
            scale = weight_ref[at : at + 1, :] * diff_ref[v, at : at + 1, :]
            store_parts(at, spread * (scale / 12.0))
        accumulate(v, cross_ref)

    @pl.loop(0, variables)
    def _(v):
        own_copy(v).wait()
        all_but_own(v, recv_sem).wait()
        relayout(v)

        @pl.when(me > 0)
        def _():
            to_low(v).start()

        @pl.when(me < n - 1)
        def _():
            to_high(v).start()

        @pl.when(me == 0)
        def _():
            x_ref[v, :, : 2 * cols] = jnp.zeros((total, 2 * cols), jnp.bfloat16)

        @pl.when(me == n - 1)
        def _():
            x_ref[v, :, (rows + 2) * cols :] = jnp.zeros((total, 2 * cols), jnp.bfloat16)

        @pl.when(v + ahead < variables)
        def _():
            send_all(v + ahead)

        @pl.when(v > 0)
        def _():
            cross(v - 1)

        gram(v)

    cross(variables - 1)

    core, chip, chips = lax.rem(me, 2), lax.div(me, 2), n // 2
    share = total // chips
    partner = me + 1 - 2 * core

    def remote(source, target, stage, device):
        return pltpu.make_async_remote_copy(
            src_ref=source,
            dst_ref=target,
            send_sem=sum_send.at[stage],
            recv_sem=sum_recv.at[stage],
            device_id={"gx": device},
            device_id_type=MESH,
        )

    swapped = remote(part_sums.at[1 - core], half, 0, partner)
    swapped.start()
    swapped.wait()
    half[...] += part_sums[core]

    def peer(k):
        return lax.rem(chip + k, chips)

    def scatter(k, carry):
        remote(half.at[pl.ds(peer(k) * share, share)], pieces.at[k - 1], 1, 2 * peer(k) + core).start()
        return carry

    lax.fori_loop(1, chips, scatter, 0)
    remote(pieces, pieces, 1, partner).wait()
    mine = pl.ds(pl.multiple_of(chip * share, share), share)
    acc = half[mine, :]
    for k in range(chips - 1):
        acc += pieces[k]
    sums_ref[core, mine, :] = acc

    def spread_out(k, carry):
        piece = sums_ref.at[core, mine]
        remote(piece, piece, 2, 2 * peer(k) + core).start()
        return carry

    lax.fori_loop(1, chips, spread_out, 0)
    others = sums_ref.at[core, pl.ds(0, total - share)]
    remote(others, others, 2, partner).wait()
    final = remote(sums_ref.at[core], sums_ref.at[core], 3, partner)
    final.start()
    final.wait_send()
    remote(sums_ref.at[1 - core], sums_ref.at[1 - core], 3, partner).wait_recv()

    for v in range(variables):
        all_but_own(v, send_sem).wait()


def gather(n, snapshots, cell_weights, diffusivity):
    own, variables, _, cols = snapshots.shape
    rows = cell_weights.shape[0]
    total = own * n
    vmem = pl.BlockSpec(memory_space=pltpu.VMEM)
    chips = n // 2
    dma = pltpu.SemaphoreType.DMA
    return pl.pallas_call(
        functools.partial(gather_kernel, n),
        out_shape=(
            jax.ShapeDtypeStruct((variables, total, (rows + 4) * cols), jnp.bfloat16),
            jax.ShapeDtypeStruct((2, total, total), jnp.float32),
        ),
        in_specs=[pl.BlockSpec(memory_space=pl.ANY), vmem, vmem],
        out_specs=(vmem, vmem),
        scratch_shapes=[
            pltpu.VMEM((total, variables, rows, cols), jnp.bfloat16),
            pltpu.VMEM((3, total, rows * cols), jnp.bfloat16),
            pltpu.VMEM((2, total, total), jnp.float32),
            pltpu.VMEM((total, total), jnp.float32),
            pltpu.VMEM((chips - 1, total // chips, total), jnp.float32),
            dma((variables,)),
            dma((variables,)),
            dma((variables,)),
            dma((2, variables)),
            dma((2, variables)),
            dma((4,)),
            dma((4,)),
        ],
        compiler_params=pltpu.CompilerParams(collective_id=0, has_side_effects=True),
        name="gather",
    )(snapshots, cell_weights, diffusivity)


def factor_kernel(cells, sums_ref, rotation_ref, reduced_ref, work):
    size = sums_ref.shape[1]
    lanes = 128
    work[:, :size] = sums_ref[0] * (1.0 / cells)
    work[:, size:] = jnp.where(iota((size, size), 0) == iota((size, size), 1), 1.0, 0.0)
    rotation_ref[...] = jnp.zeros_like(rotation_ref)
    row = iota((PIVOTS, lanes), 0)
    lane = iota((PIVOTS, lanes), 1)
    for first in range(0, size, PIVOTS):
        last = first + PIVOTS
        group, shift = first // lanes * lanes, first % lanes
        stop = size + group + lanes
        block = work[first:last, group : group + lanes]
        if shift:
            block = pltpu.roll(block, lanes - shift, 1)
        block = jnp.where(lane < PIVOTS, block, jnp.where(lane == row + PIVOTS, 1.0, 0.0))
        for base in range(0, PIVOTS, PANEL):
            columns = [
                jnp.broadcast_to(block[:, k : k + 1], (PIVOTS, lanes))
                for k in range(base, base + PANEL)
            ]
            for j in range(PANEL):
                k = base + j
                factor_of = jnp.where(row > k, columns[j] * (1.0 / columns[j][k : k + 1, :]), 0.0)
                for i in range(j + 1, PANEL):
                    columns[i] = columns[i] - factor_of * columns[i][k : k + 1, :]
                block = block - factor_of * block[k : k + 1, :]
        pivots = jnp.sum(jnp.where(lane == row, block, 0.0), axis=1, keepdims=True)
        inverse = pltpu.roll(block, lanes - PIVOTS, 1) / jnp.sqrt(pivots)
        stripe = jnp.dot(
            inverse[:, :PIVOTS],
            work[first:last, group:stop],
            precision=HIGHEST,
            preferred_element_type=jnp.float32,
        )
        rotation_ref[first:last, : group + lanes] = stripe[:, size - group :]
        if last < size:
            low = last // lanes * lanes
            work[low:, group:stop] -= lax.dot_general(
                stripe[:, low - group : size - group],
                stripe,
                TN,
                precision=HIGHEST,
                preferred_element_type=jnp.float32,
            )
    rotation = rotation_ref[...]
    turned = jnp.dot(
        rotation, sums_ref[1] * (1.0 / cells), precision=HIGHEST,
        preferred_element_type=jnp.float32,
    )
    reduced_ref[...] = lax.dot_general(
        turned, rotation, NT, precision=HIGHEST, preferred_element_type=jnp.float32
    )


def factor(cells, sums):
    size = sums.shape[1]
    vmem = pl.BlockSpec(memory_space=pltpu.VMEM)
    square = jax.ShapeDtypeStruct((size, size), jnp.float32)
    return pl.pallas_call(
        functools.partial(factor_kernel, float(cells)),
        out_shape=(square, square),
        in_specs=[vmem],
        out_specs=(vmem, vmem),
        scratch_shapes=[pltpu.VMEM((size, 2 * size), jnp.float32)],
        name="factor",
    )(sums)


def modes_kernel(rotation_ref, diff_ref, x_ref, out_ref, field, turned):
    rows, cols = diff_ref.shape[1:]
    total = rotation_ref.shape[0]
    parts = parts_of(rotation_ref[...], 3)
    lane = iota((1, cols), 1)
    masks = {
        shift: jnp.where(
            (lane >= shift) & (lane < cols + shift), -1.0 if abs(shift) == 2 else 16.0, 0.0
        )
        for shift in (-2, -1, 1, 2)
    }
    for at in range(0, (rows + 4) * cols, 2 * cols):
        right = x_ref[0, :, at : at + 2 * cols]
        acc = dot32(parts[0], right, NN)
        for part in parts[1:]:
            acc += dot32(part, right, NN)
        field[:, at : at + 2 * cols] = acc

    for at in range(rows):
        near = [field[:, (at + k) * cols : (at + k + 1) * cols] for k in range(5)]
        spread = 16.0 * (near[1] + near[3]) - (near[0] + near[4]) - 60.0 * near[2]
        for shift in (-2, -1, 1, 2):
            spread += pltpu.roll(near[2], shift % cols, 1) * masks[shift]
        spread = spread * (diff_ref[0, at : at + 1, :] / 12.0)
        turned[at] = spread.astype(jnp.bfloat16)

    swap = swap_matrix(PACK, rows)
    for g in range(0, total // PACK, 2):
        blocks = [
            turned[:, PACK * (g + h) : PACK * (g + h + 1), :].reshape(rows * PACK, cols)
            for h in range(2)
        ]
        done = dot32(swap, jnp.concatenate(blocks, axis=1), NN).astype(jnp.bfloat16)
        for h in range(2):
            out_ref[PACK * (g + h) : PACK * (g + h + 1), 0] = done[
                :, h * cols : (h + 1) * cols
            ].reshape(PACK, rows, cols)


def modes(rotation, diffusivity, fields):
    variables, rows, cols = diffusivity.shape
    total = rotation.shape[0]
    return pl.pallas_call(
        modes_kernel,
        out_shape=jax.ShapeDtypeStruct((total, variables, rows, cols), jnp.bfloat16),
        grid=(variables,),
        in_specs=[
            pl.BlockSpec((total, total), lambda v: (0, 0)),
            pl.BlockSpec((1, rows, cols), lambda v: (v, 0, 0)),
            pl.BlockSpec((1, total, (rows + 4) * cols), lambda v: (v, 0, 0)),
        ],
        out_specs=pl.BlockSpec((total, 1, rows, cols), lambda v: (0, v, 0, 0)),
        scratch_shapes=[
            pltpu.VMEM((total, (rows + 4) * cols), jnp.float32),
            pltpu.VMEM((rows, total, cols), jnp.bfloat16),
        ],
        name="modes",
    )(rotation, diffusivity, fields)


def on_device(n, snapshots, cell_weights, diffusivity):
    variables, rows, cols = diffusivity.shape
    fields, sums = gather(n, snapshots, cell_weights, diffusivity)
    rotation, reduced = factor(variables * rows * cols * n, sums)
    return modes(rotation, diffusivity, fields), reduced


def solution(mesh):
    in_specs = (
        P("gx", None, "groups", None),
        P(("groups", "gx"), None),
        P(None, ("groups", "gx"), None),
    )
    out_specs = (P(None, None, ("groups", "gx"), None), P("groups", None))
    return jax.shard_map(
        functools.partial(on_device, mesh.shape["gx"]),
        mesh=mesh, in_specs=in_specs, out_specs=out_specs, check_vma=False,
    )
```

```python
import functools

import jax
import jax.numpy as jnp
from jax import lax
from jax.experimental import pallas as pl
from jax.experimental.pallas import tpu as pltpu
from jax.sharding import PartitionSpec as P

MESH = pl.DeviceIdType.MESH
HIGHEST = lax.Precision.HIGHEST
NT = (((1,), (1,)), ((), ()))
TN = (((0,), (0,)), ((), ()))
PACK = 16
PIVOTS = 32
PANEL = 8


def iota(shape, dim):
    return lax.broadcasted_iota(jnp.int32, shape, dim)


def swap_matrix(outer, inner):
    size = outer * inner
    row, col = iota((size, size), 0), iota((size, size), 1)
    source = lax.rem(row, inner) * outer + lax.div(row, inner)
    return jnp.where(col == source, 1.0, 0.0).astype(jnp.bfloat16)


def parts_of(value, count):
    parts = []
    for _ in range(count):
        part = value.astype(jnp.bfloat16)
        parts.append(part)
        value = value - part.astype(jnp.float32)
    return parts


def dot32(a, b, dims):
    return lax.dot_general(a, b, dims, preferred_element_type=jnp.float32)


NN = (((1,), (0,)), ((), ()))


def gather_kernel(n, cells, snap_ref, weight_ref, diff_ref, field_ref, sums_ref, rotation_ref,
                  pod, x_ref, parts, part_sums, half, pieces, work, local_sem, out_sem,
                  send_sem, recv_sem, halo_send, halo_recv, sum_send, sum_recv):
    me = lax.axis_index("gx")
    own, variables, _, cols = snap_ref.shape
    total, rows = pod.shape[0], pod.shape[2]

    barrier = pltpu.get_barrier_semaphore()

    def greet(k, carry):
        pl.semaphore_signal(
            barrier, inc=1, device_id={"gx": lax.rem(me + k, n)}, device_id_type=MESH
        )
        return carry

    lax.fori_loop(1, n, greet, 0)

    def own_copy(v):
        return pltpu.make_async_copy(
            snap_ref.at[:, v, pl.ds(me * rows, rows)],
            pod.at[pl.ds(me * own, own), v],
            local_sem.at[v],
        )

    def out_copy(v):
        return pltpu.make_async_copy(x_ref.at[v], field_ref.at[v], out_sem.at[v])

    def send_all(v):
        def send(k, carry):
            offset = lax.div(k, 2) + lax.rem(k, 2) * (n // 2)
            target = lax.rem(me + offset, n)
            pltpu.make_async_remote_copy(
                src_ref=snap_ref.at[:, v, pl.ds(target * rows, rows)],
                dst_ref=pod.at[pl.ds(me * own, own), v],
                send_sem=send_sem.at[v],
                recv_sem=recv_sem.at[v],
                device_id={"gx": target},
                device_id_type=MESH,
            ).start()
            return carry

        lax.fori_loop(1, n, send, 0)

    for v in range(variables):
        own_copy(v).start()
    pl.semaphore_wait(barrier, n - 1)
    ahead = min(2, variables)
    for v in range(ahead):
        send_all(v)

    part_sums[...] = jnp.zeros_like(part_sums)
    lane_gap = iota((cols, cols), 0) - iota((cols, cols), 1)
    band = jnp.where(lane_gap == 0, -60.0, 0.0)
    band = jnp.where(jnp.abs(lane_gap) == 1, 16.0, band)
    band = jnp.where(jnp.abs(lane_gap) == 2, -1.0, band).astype(jnp.bfloat16)
    swap = swap_matrix(rows, PACK)

    def all_but_own(v, sem):
        piece = pod.at[pl.ds(0, total - own), v]
        return pltpu.make_async_copy(piece, piece, sem.at[v])

    def strip(v, first, count):
        return x_ref.at[v, :, pl.ds(first * cols, count * cols)]

    def to_low(v):
        return pltpu.make_async_remote_copy(
            src_ref=strip(v, 2, 2),
            dst_ref=strip(v, rows + 2, 2),
            send_sem=halo_send.at[0, v],
            recv_sem=halo_recv.at[0, v],
            device_id={"gx": jnp.maximum(me - 1, 0)},
            device_id_type=MESH,
        )

    def to_high(v):
        return pltpu.make_async_remote_copy(
            src_ref=strip(v, rows, 2),
            dst_ref=strip(v, 0, 2),
            send_sem=halo_send.at[1, v],
            recv_sem=halo_recv.at[1, v],
            device_id={"gx": jnp.minimum(me + 1, n - 1)},
            device_id_type=MESH,
        )

    def relayout(v):
        for g in range(0, total // PACK, 2):
            blocks = [
                pod[PACK * (g + h) : PACK * (g + h + 1), v].reshape(PACK * rows, cols)
                for h in range(2)
            ]
            turned = dot32(swap, jnp.concatenate(blocks, axis=1), NN).astype(jnp.bfloat16)
            for h in range(2):
                for at in range(rows):
                    x_ref[v, PACK * (g + h) : PACK * (g + h + 1), (at + 2) * cols : (at + 3) * cols] = (
                        turned[at * PACK : (at + 1) * PACK, h * cols : (h + 1) * cols]
                    )

    def accumulate(v, which):
        left = x_ref[v, :, 2 * cols : (rows + 2) * cols]
        acc = dot32(left, parts[0], NT)
        for p in range(1, 3):
            acc += dot32(left, parts[p], NT)
        part_sums[which, 0] += acc[:, : total // 2]
        part_sums[which, 1] += acc[:, total // 2 :]

    def store_parts(at, value):
        for p, part in enumerate(parts_of(value, 3)):
            parts[p, :, at * cols : (at + 1) * cols] = part

    def gram(v):
        for at in range(rows):
            field = x_ref[v, :, (at + 2) * cols : (at + 3) * cols].astype(jnp.float32)
            store_parts(at, field * weight_ref[at : at + 1, :])
        accumulate(v, 0)

    def cross(v):
        @pl.when(me < n - 1)
        def _():
            to_low(v).wait_recv()
            to_high(v).wait_send()

        @pl.when(me > 0)
        def _():
            to_high(v).wait_recv()
            to_low(v).wait_send()

        for at in range(rows):
            near = [x_ref[v, :, (at + k) * cols : (at + k + 1) * cols] for k in range(5)]
            wide = [near[k].astype(jnp.float32) for k in (0, 1, 3, 4)]
            spread = dot32(near[2], band, NN)
            spread += 16.0 * (wide[1] + wide[2]) - (wide[0] + wide[3])
            scale = weight_ref[at : at + 1, :] * diff_ref[v, at : at + 1, :]
            store_parts(at, spread * (scale / 12.0))
        accumulate(v, 1)
        out_copy(v).start()

    @pl.loop(0, variables)
    def _(v):
        own_copy(v).wait()
        all_but_own(v, recv_sem).wait()
        relayout(v)

        @pl.when(me > 0)
        def _():
            to_low(v).start()

        @pl.when(me < n - 1)
        def _():
            to_high(v).start()

        @pl.when(me == 0)
        def _():
            x_ref[v, :, : 2 * cols] = jnp.zeros((total, 2 * cols), jnp.bfloat16)

        @pl.when(me == n - 1)
        def _():
            x_ref[v, :, (rows + 2) * cols :] = jnp.zeros((total, 2 * cols), jnp.bfloat16)

        @pl.when(v + ahead < variables)
        def _():
            send_all(v + ahead)

        @pl.when((v > 0) & (v < variables - 1))
        def _():
            cross(v - 1)

        gram(v)

    core, chip, chips = lax.rem(me, 2), lax.div(me, 2), n // 2
    share = total // chips
    partner = me + 1 - 2 * core

    mine = pl.ds(pl.multiple_of(chip * share, share), share)

    def remote(source, target, which, stage, device):
        return pltpu.make_async_remote_copy(
            src_ref=source,
            dst_ref=target,
            send_sem=sum_send.at[which, stage],
            recv_sem=sum_recv.at[which, stage],
            device_id={"gx": device},
            device_id_type=MESH,
        )

    def peer(k):
        return lax.rem(chip + k, chips)

    def pair_up(which):
        return remote(part_sums.at[which, 1 - core], half.at[which], which, 0, partner)

    def scatter(which):
        pair_up(which).wait()
        half[which] += part_sums[which, core]

        def send(k, carry):
            piece = half.at[which, pl.ds(peer(k) * share, share)]
            remote(piece, pieces.at[which, k - 1], which, 1, 2 * peer(k) + core).start()
            return carry

        lax.fori_loop(1, chips, send, 0)

    def spread_out(which):
        remote(pieces.at[which], pieces.at[which], which, 1, partner).wait()
        acc = half[which, mine, :]
        for k in range(chips - 1):
            acc += pieces[which, k]
        sums_ref[which, core, mine, :] = acc

        def send(k, carry):
            piece = sums_ref.at[which, core, mine]
            remote(piece, piece, which, 2, 2 * peer(k) + core).start()
            return carry

        lax.fori_loop(1, chips, send, 0)

    def hand_over(which):
        others = sums_ref.at[which, core, pl.ds(0, total - share)]
        remote(others, others, which, 2, partner).wait()
        done = sums_ref.at[which, core]
        remote(done, done, which, 3, partner).start()

    def finish(which):
        sent, got = sums_ref.at[which, core], sums_ref.at[which, 1 - core]
        remote(sent, sent, which, 3, partner).wait_send()
        remote(got, got, which, 3, partner).wait_recv()

    pair_up(0).start()
    if variables > 1:
        cross(variables - 2)
    scatter(0)
    cross(variables - 1)
    pair_up(1).start()
    spread_out(0)
    hand_over(0)
    finish(0)

    stages = {1: scatter, 3: spread_out, 5: hand_over, 7: finish}
    for step in factor(cells, sums_ref, rotation_ref, work):
        if step in stages:
            stages.pop(step)(1)
    for stage in stages.values():
        stage(1)

    for v in range(variables):
        out_copy(v).wait()
        all_but_own(v, send_sem).wait()


def factor(cells, sums_ref, rotation_ref, work):
    size = rotation_ref.shape[0]
    lanes = 128
    work[:, : size // 2] = sums_ref[0, 0] * (1.0 / cells)
    work[:, size // 2 : size] = sums_ref[0, 1] * (1.0 / cells)
    work[:, size:] = jnp.where(iota((size, size), 0) == iota((size, size), 1), 1.0, 0.0)
    rotation_ref[...] = jnp.zeros_like(rotation_ref)
    row = iota((PIVOTS, lanes), 0)
    lane = iota((PIVOTS, lanes), 1)
    for first in range(0, size, PIVOTS):
        last = first + PIVOTS
        group, shift = first // lanes * lanes, first % lanes
        stop = size + group + lanes
        block = work[first:last, group : group + lanes]
        if shift:
            block = pltpu.roll(block, lanes - shift, 1)
        block = jnp.where(lane < PIVOTS, block, jnp.where(lane == row + PIVOTS, 1.0, 0.0))
        for base in range(0, PIVOTS, PANEL):
            columns = [
                jnp.broadcast_to(block[:, k : k + 1], (PIVOTS, lanes))
                for k in range(base, base + PANEL)
            ]
            for j in range(PANEL):
                k = base + j
                factor_of = jnp.where(row > k, columns[j] * (1.0 / columns[j][k : k + 1, :]), 0.0)
                for i in range(j + 1, PANEL):
                    columns[i] = columns[i] - factor_of * columns[i][k : k + 1, :]
                block = block - factor_of * block[k : k + 1, :]
        pivots = jnp.sum(jnp.where(lane == row, block, 0.0), axis=1, keepdims=True)
        inverse = pltpu.roll(block, lanes - PIVOTS, 1) / jnp.sqrt(pivots)
        stripe = jnp.dot(
            inverse[:, :PIVOTS],
            work[first:last, group:stop],
            precision=HIGHEST,
            preferred_element_type=jnp.float32,
        )
        rotation_ref[first:last, : group + lanes] = stripe[:, size - group :]
        if last < size:
            low = last // lanes * lanes
            work[low:, group:stop] -= lax.dot_general(
                stripe[:, low - group : size - group],
                stripe,
                TN,
                precision=HIGHEST,
                preferred_element_type=jnp.float32,
            )
        yield first // PIVOTS


def gather(n, cells, snapshots, cell_weights, diffusivity):
    own, variables, _, cols = snapshots.shape
    rows = cell_weights.shape[0]
    total = own * n
    vmem = pl.BlockSpec(memory_space=pltpu.VMEM)
    chips = n // 2
    dma = pltpu.SemaphoreType.DMA
    return pl.pallas_call(
        functools.partial(gather_kernel, n, float(cells)),
        out_shape=(
            jax.ShapeDtypeStruct((variables, total, (rows + 4) * cols), jnp.bfloat16),
            jax.ShapeDtypeStruct((2, 2, total, total // 2), jnp.float32),
            jax.ShapeDtypeStruct((total, total), jnp.float32),
        ),
        in_specs=[pl.BlockSpec(memory_space=pl.ANY), vmem, vmem],
        out_specs=(pl.BlockSpec(memory_space=pl.ANY), vmem, vmem),
        scratch_shapes=[
            pltpu.VMEM((total, variables, rows, cols), jnp.bfloat16),
            pltpu.VMEM((variables, total, (rows + 4) * cols), jnp.bfloat16),
            pltpu.VMEM((3, total, rows * cols), jnp.bfloat16),
            pltpu.VMEM((2, 2, total, total // 2), jnp.float32),
            pltpu.VMEM((2, total, total // 2), jnp.float32),
            pltpu.VMEM((2, chips - 1, total // chips, total // 2), jnp.float32),
            pltpu.VMEM((total, 2 * total), jnp.float32),
            dma((variables,)),
            dma((variables,)),
            dma((variables,)),
            dma((variables,)),
            dma((2, variables)),
            dma((2, variables)),
            dma((2, 4)),
            dma((2, 4)),
        ],
        compiler_params=pltpu.CompilerParams(collective_id=0, has_side_effects=True),
        name="gather",
    )(snapshots, cell_weights, diffusivity)


def modes_kernel(cells, rotation_ref, sums_ref, diff_ref, x_ref, out_ref, reduced_ref, field, turned):
    rows, cols = diff_ref.shape[1:]
    total = rotation_ref.shape[0]
    parts = parts_of(rotation_ref[...], 3)

    @pl.when(pl.program_id(0) == 0)
    def _():
        rotation = rotation_ref[...]
        cross = jnp.concatenate([sums_ref[0, 0], sums_ref[0, 1]], axis=1) * (1.0 / cells)
        product = jnp.dot(
            rotation, cross, precision=HIGHEST, preferred_element_type=jnp.float32
        )
        reduced_ref[...] = lax.dot_general(
            product, rotation, NT, precision=HIGHEST, preferred_element_type=jnp.float32
        )

    lane = iota((1, cols), 1)
    masks = {
        shift: jnp.where(
            (lane >= shift) & (lane < cols + shift), -1.0 if abs(shift) == 2 else 16.0, 0.0
        )
        for shift in (-2, -1, 1, 2)
    }
    for at in range(0, (rows + 4) * cols, 2 * cols):
        right = x_ref[0, :, at : at + 2 * cols]
        acc = dot32(parts[0], right, NN)
        for part in parts[1:]:
            acc += dot32(part, right, NN)
        field[:, at : at + 2 * cols] = acc

    for at in range(rows):
        near = [field[:, (at + k) * cols : (at + k + 1) * cols] for k in range(5)]
        spread = 16.0 * (near[1] + near[3]) - (near[0] + near[4]) - 60.0 * near[2]
        for shift in (-2, -1, 1, 2):
            spread += pltpu.roll(near[2], shift % cols, 1) * masks[shift]
        spread = spread * (diff_ref[0, at : at + 1, :] / 12.0)
        turned[at] = spread.astype(jnp.bfloat16)

    swap = swap_matrix(PACK, rows)
    for g in range(0, total // PACK, 2):
        blocks = [
            turned[:, PACK * (g + h) : PACK * (g + h + 1), :].reshape(rows * PACK, cols)
            for h in range(2)
        ]
        done = dot32(swap, jnp.concatenate(blocks, axis=1), NN).astype(jnp.bfloat16)
        for h in range(2):
            out_ref[PACK * (g + h) : PACK * (g + h + 1), 0] = done[
                :, h * cols : (h + 1) * cols
            ].reshape(PACK, rows, cols)


def modes(cells, rotation, sums, diffusivity, fields):
    variables, rows, cols = diffusivity.shape
    total = rotation.shape[0]
    return pl.pallas_call(
        functools.partial(modes_kernel, float(cells)),
        out_shape=(
            jax.ShapeDtypeStruct((total, variables, rows, cols), jnp.bfloat16),
            jax.ShapeDtypeStruct((total, total), jnp.float32),
        ),
        grid=(variables,),
        in_specs=[
            pl.BlockSpec((total, total), lambda v: (0, 0)),
            pl.BlockSpec((1, 2, total, total // 2), lambda v: (1, 0, 0, 0)),
            pl.BlockSpec((1, rows, cols), lambda v: (v, 0, 0)),
            pl.BlockSpec((1, total, (rows + 4) * cols), lambda v: (v, 0, 0)),
        ],
        out_specs=(
            pl.BlockSpec((total, 1, rows, cols), lambda v: (0, v, 0, 0)),
            pl.BlockSpec((total, total), lambda v: (0, 0)),
        ),
        scratch_shapes=[
            pltpu.VMEM((total, (rows + 4) * cols), jnp.float32),
            pltpu.VMEM((rows, total, cols), jnp.bfloat16),
        ],
        name="modes",
    )(rotation, sums, diffusivity, fields)


def on_device(n, snapshots, cell_weights, diffusivity):
    variables, rows, cols = diffusivity.shape
    cells = variables * rows * cols * n
    fields, sums, rotation = gather(n, cells, snapshots, cell_weights, diffusivity)
    return modes(cells, rotation, sums, diffusivity, fields)


def solution(mesh):
    in_specs = (
        P("gx", None, "groups", None),
        P(("groups", "gx"), None),
        P(None, ("groups", "gx"), None),
    )
    out_specs = (P(None, None, ("groups", "gx"), None), P("groups", None))
    return jax.shard_map(
        functools.partial(on_device, mesh.shape["gx"]),
        mesh=mesh, in_specs=in_specs, out_specs=out_specs, check_vma=False,
    )
```

```python
import functools

import jax
import jax.numpy as jnp
from jax import lax
from jax.experimental import pallas as pl
from jax.experimental.pallas import tpu as pltpu
from jax.sharding import PartitionSpec as P

MESH = pl.DeviceIdType.MESH
HIGHEST = lax.Precision.HIGHEST
NT = (((1,), (1,)), ((), ()))
TN = (((0,), (0,)), ((), ()))
PACK = 16
PIVOTS = 32
PANEL = 8


def iota(shape, dim):
    return lax.broadcasted_iota(jnp.int32, shape, dim)


def swap_matrix(outer, inner):
    size = outer * inner
    row, col = iota((size, size), 0), iota((size, size), 1)
    source = lax.rem(row, inner) * outer + lax.div(row, inner)
    return jnp.where(col == source, 1.0, 0.0).astype(jnp.bfloat16)


def parts_of(value, count):
    parts = []
    for _ in range(count):
        part = value.astype(jnp.bfloat16)
        parts.append(part)
        value = value - part.astype(jnp.float32)
    return parts


def dot32(a, b, dims):
    return lax.dot_general(a, b, dims, preferred_element_type=jnp.float32)


NN = (((1,), (0,)), ((), ()))


def gather_kernel(n, cells, snap_ref, weight_ref, diff_ref, field_ref, sums_ref, rotation_ref,
                  pod, x_ref, parts, part_sums, half, pieces, work, local_sem, out_sem,
                  send_sem, recv_sem, halo_send, halo_recv, sum_send, sum_recv):
    me = lax.axis_index("gx")
    own, variables, _, cols = snap_ref.shape
    total, rows = pod.shape[0], pod.shape[2]

    barrier = pltpu.get_barrier_semaphore()

    def greet(k, carry):
        pl.semaphore_signal(
            barrier, inc=1, device_id={"gx": lax.rem(me + k, n)}, device_id_type=MESH
        )
        return carry

    lax.fori_loop(1, n, greet, 0)

    def own_copy(v):
        return pltpu.make_async_copy(
            snap_ref.at[:, v, pl.ds(me * rows, rows)],
            pod.at[pl.ds(me * own, own), v],
            local_sem.at[v],
        )

    def out_copy(v):
        return pltpu.make_async_copy(x_ref.at[v], field_ref.at[v], out_sem.at[v])

    def send_all(v):
        def send(k, carry):
            offset = lax.div(k, 2) + lax.rem(k, 2) * (n // 2)
            target = lax.rem(me + offset, n)
            pltpu.make_async_remote_copy(
                src_ref=snap_ref.at[:, v, pl.ds(target * rows, rows)],
                dst_ref=pod.at[pl.ds(me * own, own), v],
                send_sem=send_sem.at[v],
                recv_sem=recv_sem.at[v],
                device_id={"gx": target},
                device_id_type=MESH,
            ).start()
            return carry

        lax.fori_loop(1, n, send, 0)

    for v in range(variables):
        own_copy(v).start()
    pl.semaphore_wait(barrier, n - 1)
    ahead = min(2, variables)
    for v in range(ahead):
        send_all(v)

    part_sums[...] = jnp.zeros_like(part_sums)
    lane_gap = iota((cols, cols), 0) - iota((cols, cols), 1)
    band = jnp.where(lane_gap == 0, -60.0, 0.0)
    band = jnp.where(jnp.abs(lane_gap) == 1, 16.0, band)
    band = jnp.where(jnp.abs(lane_gap) == 2, -1.0, band).astype(jnp.bfloat16)
    swap = swap_matrix(rows, PACK)

    def all_but_own(v, sem):
        piece = pod.at[pl.ds(0, total - own), v]
        return pltpu.make_async_copy(piece, piece, sem.at[v])

    def strip(v, first, count):
        return x_ref.at[v, :, pl.ds(first * cols, count * cols)]

    def to_low(v):
        return pltpu.make_async_remote_copy(
            src_ref=strip(v, 2, 2),
            dst_ref=strip(v, rows + 2, 2),
            send_sem=halo_send.at[0, v],
            recv_sem=halo_recv.at[0, v],
            device_id={"gx": jnp.maximum(me - 1, 0)},
            device_id_type=MESH,
        )

    def to_high(v):
        return pltpu.make_async_remote_copy(
            src_ref=strip(v, rows, 2),
            dst_ref=strip(v, 0, 2),
            send_sem=halo_send.at[1, v],
            recv_sem=halo_recv.at[1, v],
            device_id={"gx": jnp.minimum(me + 1, n - 1)},
            device_id_type=MESH,
        )

    def relayout(v):
        for g in range(0, total // PACK, 2):
            blocks = [
                pod[PACK * (g + h) : PACK * (g + h + 1), v].reshape(PACK * rows, cols)
                for h in range(2)
            ]
            turned = dot32(swap, jnp.concatenate(blocks, axis=1), NN).astype(jnp.bfloat16)
            for h in range(2):
                for at in range(rows):
                    x_ref[v, PACK * (g + h) : PACK * (g + h + 1), (at + 2) * cols : (at + 3) * cols] = (
                        turned[at * PACK : (at + 1) * PACK, h * cols : (h + 1) * cols]
                    )

    def accumulate(v, which, count):
        left = x_ref[v, :, 2 * cols : (rows + 2) * cols]
        acc = dot32(left, parts[0], NT)
        for p in range(1, count):
            acc += dot32(left, parts[p], NT)
        part_sums[which, 0] += acc[:, : total // 2]
        part_sums[which, 1] += acc[:, total // 2 :]

    def store_parts(at, value, count):
        for p, part in enumerate(parts_of(value, count)):
            parts[p, :, at * cols : (at + 1) * cols] = part

    def gram(v):
        for at in range(rows):
            field = x_ref[v, :, (at + 2) * cols : (at + 3) * cols].astype(jnp.float32)
            store_parts(at, field * weight_ref[at : at + 1, :], 3)
        accumulate(v, 0, 3)

    def cross(v):
        @pl.when(me < n - 1)
        def _():
            to_low(v).wait_recv()
            to_high(v).wait_send()

        @pl.when(me > 0)
        def _():
            to_high(v).wait_recv()
            to_low(v).wait_send()

        for at in range(rows):
            near = [x_ref[v, :, (at + k) * cols : (at + k + 1) * cols] for k in range(5)]
            wide = [near[k].astype(jnp.float32) for k in (0, 1, 3, 4)]
            spread = dot32(near[2], band, NN)
            spread += 16.0 * (wide[1] + wide[2]) - (wide[0] + wide[3])
            scale = weight_ref[at : at + 1, :] * diff_ref[v, at : at + 1, :]
            store_parts(at, spread * (scale / 12.0), 2)
        accumulate(v, 1, 2)
        out_copy(v).start()

    @pl.loop(0, variables)
    def _(v):
        own_copy(v).wait()
        all_but_own(v, recv_sem).wait()
        relayout(v)

        @pl.when(me > 0)
        def _():
            to_low(v).start()

        @pl.when(me < n - 1)
        def _():
            to_high(v).start()

        @pl.when(me == 0)
        def _():
            x_ref[v, :, : 2 * cols] = jnp.zeros((total, 2 * cols), jnp.bfloat16)

        @pl.when(me == n - 1)
        def _():
            x_ref[v, :, (rows + 2) * cols :] = jnp.zeros((total, 2 * cols), jnp.bfloat16)

        @pl.when(v + ahead < variables)
        def _():
            send_all(v + ahead)

        @pl.when((v > 0) & (v < variables - 1))
        def _():
            cross(v - 1)

        gram(v)

    core, chip, chips = lax.rem(me, 2), lax.div(me, 2), n // 2
    share = total // chips
    partner = me + 1 - 2 * core

    mine = pl.ds(pl.multiple_of(chip * share, share), share)

    def remote(source, target, which, stage, device):
        return pltpu.make_async_remote_copy(
            src_ref=source,
            dst_ref=target,
            send_sem=sum_send.at[which, stage],
            recv_sem=sum_recv.at[which, stage],
            device_id={"gx": device},
            device_id_type=MESH,
        )

    def peer(k):
        return lax.rem(chip + k, chips)

    def pair_up(which):
        return remote(part_sums.at[which, 1 - core], half.at[which], which, 0, partner)

    def scatter(which):
        pair_up(which).wait()
        half[which] += part_sums[which, core]

        def send(k, carry):
            piece = half.at[which, pl.ds(peer(k) * share, share)]
            remote(piece, pieces.at[which, k - 1], which, 1, 2 * peer(k) + core).start()
            return carry

        lax.fori_loop(1, chips, send, 0)

    def spread_out(which):
        remote(pieces.at[which], pieces.at[which], which, 1, partner).wait()
        acc = half[which, mine, :]
        for k in range(chips - 1):
            acc += pieces[which, k]
        sums_ref[which, core, mine, :] = acc

        def send(k, carry):
            piece = sums_ref.at[which, core, mine]
            remote(piece, piece, which, 2, 2 * peer(k) + core).start()
            return carry

        lax.fori_loop(1, chips, send, 0)

    def hand_over(which):
        others = sums_ref.at[which, core, pl.ds(0, total - share)]
        remote(others, others, which, 2, partner).wait()
        done = sums_ref.at[which, core]
        remote(done, done, which, 3, partner).start()

    def finish(which):
        sent, got = sums_ref.at[which, core], sums_ref.at[which, 1 - core]
        remote(sent, sent, which, 3, partner).wait_send()
        remote(got, got, which, 3, partner).wait_recv()

    pair_up(0).start()
    if variables > 1:
        cross(variables - 2)
    scatter(0)
    cross(variables - 1)
    pair_up(1).start()
    spread_out(0)
    hand_over(0)
    finish(0)

    stages = {1: scatter, 3: spread_out, 5: hand_over, 7: finish}
    for step in factor(cells, sums_ref, rotation_ref, work):
        if step in stages:
            stages.pop(step)(1)
    for stage in stages.values():
        stage(1)

    for v in range(variables):
        out_copy(v).wait()
        all_but_own(v, send_sem).wait()


def factor(cells, sums_ref, rotation_ref, work):
    size = rotation_ref.shape[0]
    lanes = 128
    work[:, : size // 2] = sums_ref[0, 0] * (1.0 / cells)
    work[:, size // 2 : size] = sums_ref[0, 1] * (1.0 / cells)
    work[:, size:] = jnp.where(iota((size, size), 0) == iota((size, size), 1), 1.0, 0.0)
    rotation_ref[...] = jnp.zeros_like(rotation_ref)
    row = iota((PIVOTS, lanes), 0)
    lane = iota((PIVOTS, lanes), 1)
    for first in range(0, size, PIVOTS):
        last = first + PIVOTS
        group, shift = first // lanes * lanes, first % lanes
        stop = size + group + lanes
        block = work[first:last, group : group + lanes]
        if shift:
            block = pltpu.roll(block, lanes - shift, 1)
        block = jnp.where(lane < PIVOTS, block, jnp.where(lane == row + PIVOTS, 1.0, 0.0))
        for base in range(0, PIVOTS, PANEL):
            columns = [
                jnp.broadcast_to(block[:, k : k + 1], (PIVOTS, lanes))
                for k in range(base, base + PANEL)
            ]
            for j in range(PANEL):
                k = base + j
                factor_of = jnp.where(row > k, columns[j] * (1.0 / columns[j][k : k + 1, :]), 0.0)
                for i in range(j + 1, PANEL):
                    columns[i] = columns[i] - factor_of * columns[i][k : k + 1, :]
                block = block - factor_of * block[k : k + 1, :]
        pivots = jnp.sum(jnp.where(lane == row, block, 0.0), axis=1, keepdims=True)
        inverse = pltpu.roll(block, lanes - PIVOTS, 1) / jnp.sqrt(pivots)
        stripe = jnp.dot(
            inverse[:, :PIVOTS],
            work[first:last, group:stop],
            precision=HIGHEST,
            preferred_element_type=jnp.float32,
        )
        rotation_ref[first:last, : group + lanes] = stripe[:, size - group :]
        if last < size:
            low = last // lanes * lanes
            work[low:, group:stop] -= lax.dot_general(
                stripe[:, low - group : size - group],
                stripe,
                TN,
                precision=HIGHEST,
                preferred_element_type=jnp.float32,
            )
        yield first // PIVOTS


def gather(n, cells, snapshots, cell_weights, diffusivity):
    own, variables, _, cols = snapshots.shape
    rows = cell_weights.shape[0]
    total = own * n
    vmem = pl.BlockSpec(memory_space=pltpu.VMEM)
    chips = n // 2
    dma = pltpu.SemaphoreType.DMA
    return pl.pallas_call(
        functools.partial(gather_kernel, n, float(cells)),
        out_shape=(
            jax.ShapeDtypeStruct((variables, total, (rows + 4) * cols), jnp.bfloat16),
            jax.ShapeDtypeStruct((2, 2, total, total // 2), jnp.float32),
            jax.ShapeDtypeStruct((total, total), jnp.float32),
        ),
        in_specs=[pl.BlockSpec(memory_space=pl.ANY), vmem, vmem],
        out_specs=(pl.BlockSpec(memory_space=pl.ANY), vmem, vmem),
        scratch_shapes=[
            pltpu.VMEM((total, variables, rows, cols), jnp.bfloat16),
            pltpu.VMEM((variables, total, (rows + 4) * cols), jnp.bfloat16),
            pltpu.VMEM((3, total, rows * cols), jnp.bfloat16),
            pltpu.VMEM((2, 2, total, total // 2), jnp.float32),
            pltpu.VMEM((2, total, total // 2), jnp.float32),
            pltpu.VMEM((2, chips - 1, total // chips, total // 2), jnp.float32),
            pltpu.VMEM((total, 2 * total), jnp.float32),
            dma((variables,)),
            dma((variables,)),
            dma((variables,)),
            dma((variables,)),
            dma((2, variables)),
            dma((2, variables)),
            dma((2, 4)),
            dma((2, 4)),
        ],
        compiler_params=pltpu.CompilerParams(collective_id=0, has_side_effects=True),
        name="gather",
    )(snapshots, cell_weights, diffusivity)


def modes_kernel(cells, rotation_ref, sums_ref, diff_ref, x_ref, out_ref, reduced_ref, field, turned):
    rows, cols = diff_ref.shape[1:]
    total = rotation_ref.shape[0]
    parts = parts_of(rotation_ref[...], 3)

    @pl.when(pl.program_id(0) == 0)
    def _():
        rotation = rotation_ref[...]
        cross = jnp.concatenate([sums_ref[0, 0], sums_ref[0, 1]], axis=1) * (1.0 / cells)
        product = jnp.dot(
            rotation, cross, precision=HIGHEST, preferred_element_type=jnp.float32
        )
        reduced_ref[...] = lax.dot_general(
            product, rotation, NT, precision=HIGHEST, preferred_element_type=jnp.float32
        )

    lane = iota((1, cols), 1)
    masks = {
        shift: jnp.where(
            (lane >= shift) & (lane < cols + shift), -1.0 if abs(shift) == 2 else 16.0, 0.0
        )
        for shift in (-2, -1, 1, 2)
    }
    for at in range(0, (rows + 4) * cols, 2 * cols):
        right = x_ref[0, :, at : at + 2 * cols]
        acc = dot32(parts[0], right, NN)
        for part in parts[1:]:
            acc += dot32(part, right, NN)
        field[:, at : at + 2 * cols] = acc

    for at in range(rows):
        near = [field[:, (at + k) * cols : (at + k + 1) * cols] for k in range(5)]
        spread = 16.0 * (near[1] + near[3]) - (near[0] + near[4]) - 60.0 * near[2]
        for shift in (-2, -1, 1, 2):
            spread += pltpu.roll(near[2], shift % cols, 1) * masks[shift]
        spread = spread * (diff_ref[0, at : at + 1, :] / 12.0)
        turned[at] = spread.astype(jnp.bfloat16)

    swap = swap_matrix(PACK, rows)
    for g in range(0, total // PACK, 2):
        blocks = [
            turned[:, PACK * (g + h) : PACK * (g + h + 1), :].reshape(rows * PACK, cols)
            for h in range(2)
        ]
        done = dot32(swap, jnp.concatenate(blocks, axis=1), NN).astype(jnp.bfloat16)
        for h in range(2):
            out_ref[PACK * (g + h) : PACK * (g + h + 1), 0] = done[
                :, h * cols : (h + 1) * cols
            ].reshape(PACK, rows, cols)


def modes(cells, rotation, sums, diffusivity, fields):
    variables, rows, cols = diffusivity.shape
    total = rotation.shape[0]
    return pl.pallas_call(
        functools.partial(modes_kernel, float(cells)),
        out_shape=(
            jax.ShapeDtypeStruct((total, variables, rows, cols), jnp.bfloat16),
            jax.ShapeDtypeStruct((total, total), jnp.float32),
        ),
        grid=(variables,),
        in_specs=[
            pl.BlockSpec((total, total), lambda v: (0, 0)),
            pl.BlockSpec((1, 2, total, total // 2), lambda v: (1, 0, 0, 0)),
            pl.BlockSpec((1, rows, cols), lambda v: (v, 0, 0)),
            pl.BlockSpec((1, total, (rows + 4) * cols), lambda v: (v, 0, 0)),
        ],
        out_specs=(
            pl.BlockSpec((total, 1, rows, cols), lambda v: (0, v, 0, 0)),
            pl.BlockSpec((total, total), lambda v: (0, 0)),
        ),
        scratch_shapes=[
            pltpu.VMEM((total, (rows + 4) * cols), jnp.float32),
            pltpu.VMEM((rows, total, cols), jnp.bfloat16),
        ],
        name="modes",
    )(rotation, sums, diffusivity, fields)


def on_device(n, snapshots, cell_weights, diffusivity):
    variables, rows, cols = diffusivity.shape
    cells = variables * rows * cols * n
    fields, sums, rotation = gather(n, cells, snapshots, cell_weights, diffusivity)
    return modes(cells, rotation, sums, diffusivity, fields)


def solution(mesh):
    in_specs = (
        P("gx", None, "groups", None),
        P(("groups", "gx"), None),
        P(None, ("groups", "gx"), None),
    )
    out_specs = (P(None, None, ("groups", "gx"), None), P("groups", None))
    return jax.shard_map(
        functools.partial(on_device, mesh.shape["gx"]),
        mesh=mesh, in_specs=in_specs, out_specs=out_specs, check_vma=False,
    )
```
